32 devices in a mesh: seq: 8 (over z, x), tensor: 4 (over y, core).
Axes of the slice: x: 2, y: 2, z: 4, core: 2. Of those that a mesh axis runs over, the one named last changes fastest.
Arguments:
- queries: bfloat16 [8192, 8192], P('seq', 'tensor'), may hold values from -6 to 6
- keys: bfloat16 [8192, 1024], P('seq', 'tensor'), may hold values from -6 to 6
- values: bfloat16 [8192, 1024], P('seq', 'tensor'), may hold values from -6 to 6
- key_blocks: int32 [64, 64, 16], P('tensor'), may hold values from 0 to 63, as said below
- block_counts: int32 [64, 64], P('tensor'), may hold values from 1 to 16, as said below
- out_weight: bfloat16 [8192, 8192], P('tensor'), may hold values from -0.59765625 to 0.59765625
Outputs:
- projected: bfloat16 [8192, 8192], P('seq', 'tensor')
The draws below stay inside these ranges and needn't reach their ends.
Inputs may be any that keep to these rules, and one draw needn't show every extreme that they name: For head h and query block b the first block_counts[h, b] entries of key_blocks[h, b] are different blocks of 0 to b, the first being b itself; the later entries are block numbers without meaning. block_counts[h, b] is at most b + 1; the last query block of every head has exactly 16.
All inputs are finite; a program needn't handle non-finite values.
Results may differ from the reference program's by a relative error of at most 0.014.
Values may be sent and summed in bfloat16 or wider, within the bound.
A program may use at most 128 MiB of HBM per device.

```python
import jax
import jax.numpy as jnp
from jax import lax

D = 8192
HEADS = 64
KV_HEADS = 8
HEAD_DIM = 128
BLOCK = 128
KMAX = 16
SEQ = 8192
NB = 64
HQ_DEV = 16
N_TENSOR = 4


def draw_queries(key, part):
    base = jnp.clip(jax.random.normal(jax.random.fold_in(key, 1), (SEQ, HEADS * HEAD_DIM), jnp.float32), -6.0, 6.0)
    return base.astype(jnp.bfloat16)


def draw_keys(key, part):
    base = jnp.clip(jax.random.normal(jax.random.fold_in(key, 3), (SEQ, KV_HEADS * HEAD_DIM), jnp.float32), -6.0, 6.0)
    return base.astype(jnp.bfloat16)


def mask_layout(key):
    base = jax.random.fold_in(key, 29)
    rows = jnp.arange(NB, dtype=jnp.int32)
    density = jax.random.randint(jax.random.fold_in(base, 1), (HEADS, 1), 1, 5)
    cap = 1 + (KMAX - 1) * (rows[None, :] + 1) * density // (NB * 4)
    low = jnp.maximum(1, cap // 2)
    counts = jax.random.randint(jax.random.fold_in(base, 2), (HEADS, NB), low, cap + 1)
    counts = jnp.minimum(counts, rows[None, :] + 1)
    counts = jnp.where(rows[None, :] == NB - 1, KMAX, counts).astype(jnp.int32)
    kind = jax.random.randint(jax.random.fold_in(base, 3), (HEADS, 1, 1), 0, 2)
    vertical = jax.random.randint(jax.random.fold_in(base, 4), (HEADS, 1, NB), 0, 4) == 0
    slash_set = jax.random.randint(jax.random.fold_in(base, 5), (HEADS, NB), 0, 4) == 0
    slash_set = slash_set | (rows[None, :] == 1)
    offsets = jnp.mod(rows[:, None] - rows[None, :], NB)
    slash_hit = slash_set[:, offsets]
    scattered = jax.random.randint(jax.random.fold_in(base, 6), (HEADS, NB, NB), 0, 3) == 0
    noise = jax.random.randint(jax.random.fold_in(base, 7), (HEADS, NB, NB), 0, 1000)
    pattern = jnp.where(kind == 0, 2000 * vertical.astype(jnp.int32) + 2000 * slash_hit.astype(jnp.int32), 2000 * scattered.astype(jnp.int32))
    valid = (rows[None, None, :] <= rows[None, :, None]).astype(jnp.int32)
    diagonal = (rows[None, None, :] == rows[None, :, None]).astype(jnp.int32)
    score = valid * (200000 + noise + pattern) + diagonal * 200000
    distinct = score * NB + rows[None, None, :]
    slots = lax.top_k(distinct, KMAX)[1].astype(jnp.int32)
    return (slots, counts)


def draw_key_blocks(key, part):
    return mask_layout(key)[0]


def draw_block_counts(key, part):
    return mask_layout(key)[1]


def with_spikes(entries, key, source, target, blocks, factor):
    def block_of(position):
        return (jnp.arange(entries.shape[position]) // (entries.shape[position] // blocks)).reshape((-1,) + (1,) * (entries.ndim - 1 - position))

    one_side = jax.random.permutation(key, blocks)[block_of(target)]
    second = (block_of(target) + blocks // 2) % blocks
    return jnp.where((block_of(source) == one_side) | (block_of(source) == second), factor * entries, entries)


def block_scale(own_key, dims, split, smallest, high):
    loudness = 1.0
    for dim, blocks in split:
        heights = jax.random.uniform(jax.random.fold_in(jax.random.fold_in(own_key, 6), dim), (blocks,), jnp.float32, smallest / len(split), high / len(split))
        loudness = loudness * jnp.repeat(jnp.exp(heights), dims[dim] // blocks).reshape((-1,) + (1,) * (len(dims) - 1 - dim))
    return loudness


def centred(own_key, shape, deviation, bound, split=(), kind=jnp.bfloat16):
    factor_of = block_scale(own_key, shape, split, -0.22, 0.18) if split else 1.0
    result = jax.random.normal(own_key, shape, jnp.float32) * deviation * factor_of
    return jnp.minimum(jnp.maximum(result, -bound), bound).astype(kind)


def noise_with(own_key, dims, deviation, limit, pieces, heavy, held_as=jnp.bfloat16):
    array = deviation * jax.random.normal(own_key, dims, jnp.float32)
    if pieces:
        array = array * block_scale(own_key, dims, pieces, -0.22, 0.18)
    return jnp.clip(with_spikes(array, jax.random.fold_in(own_key, 3), *heavy), -limit, limit).astype(held_as)


def setup_inputs(seed: int = 0) -> dict:
    splits = jax.random.split(jax.random.key(seed), 7)
    queries = draw_queries(jax.random.fold_in(splits[6], 71), 0)
    keys = draw_keys(jax.random.fold_in(splits[6], 71), 0)
    values = centred(splits[2], (SEQ, KV_HEADS * HEAD_DIM), 1.0, 6.0, ((0, 8), (1, 4)))
    key_blocks = draw_key_blocks(jax.random.fold_in(splits[6], 71), 0)
    block_counts = draw_block_counts(jax.random.fold_in(splits[6], 71), 0)
    out_weight = noise_with(splits[5], (HEADS * HEAD_DIM, D), 0.1, 0.59765625, ((0, 4),), (0, 1, 4, 2.0))
    return {"queries": queries, "keys": keys, "values": values, "key_blocks": key_blocks, "block_counts": block_counts, "out_weight": out_weight}


neg_large = -1.0e30


def reference(queries, keys, values, key_blocks, block_counts, out_weight):
    seq_len = queries.shape[0]
    nblocks = seq_len // BLOCK
    ratio = HEADS // KV_HEADS
    softmax_scale = HEAD_DIM ** -0.5
    q_all = queries.reshape(nblocks, BLOCK, HEADS, HEAD_DIM)
    k_all = keys.reshape(nblocks, BLOCK, KV_HEADS, HEAD_DIM)
    v_all = values.reshape(nblocks, BLOCK, KV_HEADS, HEAD_DIM)
    q_pos = jnp.arange(BLOCK, dtype=jnp.int32)[:, None]
    k_pos = jnp.arange(BLOCK, dtype=jnp.int32)[None, :]
    block_ids = jnp.arange(nblocks, dtype=jnp.int32)
    slot_ids = jnp.arange(KMAX, dtype=jnp.int32)

    def one_head(head):
        group = head // ratio
        query_per_head = lax.dynamic_index_in_dim(q_all, head, 2, keepdims=False).astype(jnp.float32)
        k_head = lax.dynamic_index_in_dim(k_all, group, 2, keepdims=False).astype(jnp.float32)
        v_head = lax.dynamic_index_in_dim(v_all, group, 2, keepdims=False).astype(jnp.float32)
        slots = lax.dynamic_index_in_dim(key_blocks, head, 0, keepdims=False)
        counts = lax.dynamic_index_in_dim(block_counts, head, 0, keepdims=False)
        selected_key_rows = k_head[slots]
        selected_value_rows = v_head[slots]
        logit_scores = jnp.einsum("imh,itzh->imtz", query_per_head, selected_key_rows) * softmax_scale
        slot_used = slot_ids[None, :] < counts[:, None]
        earlier = slots < block_ids[:, None]
        visible = slot_used[:, None, :, None] & (earlier[:, None, :, None] | (q_pos >= k_pos)[None, :, None, :])
        masked = jnp.where(visible, logit_scores, neg_large)
        top = jnp.max(masked, axis=(2, 3))
        weights = jnp.where(visible, jnp.exp(masked - top[:, :, None, None]), 0.0)
        total = jnp.sum(weights, axis=(2, 3))
        rounded_output = lax.optimization_barrier(weights.astype(jnp.bfloat16)).astype(jnp.float32)
        summed_heads = jnp.einsum("xuin,xinw->xuw", rounded_output, selected_value_rows)
        return (summed_heads / total[:, :, None]).astype(jnp.bfloat16)

    attended = lax.map(one_head, jnp.arange(HEADS, dtype=jnp.int32))
    attended = attended.transpose(1, 2, 0, 3).reshape(seq_len, HEADS * HEAD_DIM)
    width = HQ_DEV * HEAD_DIM
    groups = attended.reshape(seq_len, N_TENSOR, width).transpose(1, 0, 2)
    weight_groups = out_weight.reshape(N_TENSOR, width, D)

    def add_group(total, pair):
        part = jnp.dot(pair[0], pair[1], preferred_element_type=jnp.float32)
        part = lax.optimization_barrier(part.astype(jnp.bfloat16)).astype(jnp.float32)
        return total + part, None

    summed_heads, _ = lax.scan(add_group, jnp.zeros((seq_len, D), jnp.float32), (groups, weight_groups))
    return summed_heads.astype(jnp.bfloat16)
```

```python
import functools

import jax
import jax.numpy as jnp
from jax import lax
from jax.experimental import pallas as pl
from jax.experimental.pallas import tpu as pltpu
from jax.sharding import PartitionSpec as P

HEAD_DIM = 128
BLOCK = 128
LOG2E = 1.4426950408889634
NEG = -1e30
PAIR = 2
STEP = 2


def attend_kernel(order_ref, count_ref, slot_ref, q_ref, k_ref, v_ref, o_ref, *, units, blocks, kmax):
    coef = HEAD_DIM ** (-0.5) * LOG2E
    key_pos = lax.broadcasted_iota(jnp.int32, (BLOCK, BLOCK), 0)
    query_pos = lax.broadcasted_iota(jnp.int32, (BLOCK, BLOCK), 1)
    causal = key_pos <= query_pos

    def run(first, depth):
        sets = []
        for side in range(PAIR):
            unit = order_ref[first + side]
            count = count_ref[unit]
            head = unit // blocks
            block = unit % blocks
            rows = pl.ds(pl.multiple_of(block * BLOCK, BLOCK), BLOCK)
            cols = pl.ds(pl.multiple_of(head * HEAD_DIM, HEAD_DIM), HEAD_DIM)
            own = slot_ref[unit * kmax]
            chosen = [own]
            for slot in range(1, depth):
                chosen.append(jnp.where(slot < count, slot_ref[unit * kmax + slot], own))
            sets.append((count, rows, cols, chosen))
        scored = []
        for count, rows, cols, chosen in sets:
            q = q_ref[rows, cols]
            scores = []
            top = None
            for slot in range(depth):
                start = pl.multiple_of(chosen[slot] * BLOCK, BLOCK)
                s = lax.dot_general(
                    k_ref[pl.ds(start, BLOCK), :], q, (((1,), (1,)), ((), ())),
                    preferred_element_type=jnp.float32,
                )
                if slot == 0:
                    s = jnp.where(causal, s, NEG)
                else:
                    s = jnp.where(slot < count, s, NEG)
                scores.append(s)
                part = jnp.max(s.reshape(BLOCK // 8, 8, BLOCK), axis=0)
                top = part if top is None else jnp.maximum(top, part)
            scored.append((scores, jnp.max(top, axis=0, keepdims=True) * coef))
        for (count, rows, cols, chosen), (scores, top) in zip(sets, scored):
            acc = None
            total = None
            for slot in range(0, depth, 2):
                n = min(2, depth - slot)
                probs = [jnp.exp2(scores[slot + i] * coef - top) for i in range(n)]
                for p in probs:
                    part = jnp.sum(p.reshape(BLOCK // 8, 8, BLOCK), axis=0)
                    total = part if total is None else total + part
                vals = [v_ref[chosen[slot + i]] for i in range(n)]
                if n == 2:
                    lhs = jnp.concatenate(vals, axis=1)
                    rhs = jnp.concatenate([p.astype(jnp.bfloat16) for p in probs], axis=0)
                else:
                    lhs, rhs = vals[0], probs[0].astype(jnp.bfloat16)
                term = jnp.dot(lhs, rhs, preferred_element_type=jnp.float32)
                acc = term if acc is None else acc + term
            out = acc / jnp.sum(total, axis=0, keepdims=True)
            o_ref[rows, cols] = out.T.astype(jnp.bfloat16)

    def loop(index, carry):
        first = index * PAIR
        most = count_ref[order_ref[first + PAIR - 1]]
        below = 0
        for depth in range(STEP, kmax + STEP, STEP):
            depth = min(depth, kmax)

            @pl.when((most > below) & (most <= depth))
            def _(depth=depth):
                run(first, depth)

            below = depth
        return carry

    lax.fori_loop(0, units // PAIR, loop, 0)


def attend(queries, key_head, value_head, slots, counts, column):
    tokens = queries.shape[0]
    heads, blocks, kmax = slots.shape
    width = heads * HEAD_DIM
    units = heads * blocks
    flat = counts.reshape(units)
    order = jnp.argsort(flat).astype(jnp.int32)
    smem = pl.BlockSpec(memory_space=pltpu.SMEM)
    return pl.pallas_call(
        functools.partial(attend_kernel, units=units, blocks=blocks, kmax=kmax),
        out_shape=jax.ShapeDtypeStruct((tokens, width), jnp.bfloat16),
        grid=(1,),
        in_specs=[
            smem,
            smem,
            smem,
            pl.BlockSpec((tokens, width), lambda i: (0, column)),
            pl.BlockSpec(key_head.shape, lambda i: (0, 0)),
            pl.BlockSpec(value_head.shape, lambda i: (0, 0, 0)),
        ],
        out_specs=pl.BlockSpec((tokens, width), lambda i: (0, 0)),
        compiler_params=pltpu.CompilerParams(vmem_limit_bytes=48 << 20),
        cost_estimate=pl.CostEstimate(flops=units * 8 * 4 * BLOCK**3, bytes_accessed=8 << 20, transcendentals=0),
        name="attend",
    )(order, flat, slots.reshape(-1), queries, key_head, value_head)


def project_kernel(*refs):
    lhs, (w_ref, o_ref) = refs[:-2], refs[-2:]
    acc = None
    at = 0
    for ref in lhs:
        depth = ref.shape[1]
        term = jnp.dot(ref[...], w_ref[at : at + depth, :], preferred_element_type=jnp.float32)
        acc = term if acc is None else acc + term
        at += depth
    o_ref[0] = acc.astype(jnp.bfloat16)


def project(parts, out_weight, groups):
    tokens = parts[0].shape[0]
    depth, features = out_weight.shape
    width = features // groups
    tile = min(512, width)
    per = width // tile
    return pl.pallas_call(
        project_kernel,
        out_shape=jax.ShapeDtypeStruct((groups, tokens, width), jnp.bfloat16),
        grid=(groups, per),
        in_specs=[pl.BlockSpec(p.shape, lambda g, i: (0, 0)) for p in parts]
        + [pl.BlockSpec((depth, tile), lambda g, i: (0, g * per + i))],
        out_specs=pl.BlockSpec((1, tokens, tile), lambda g, i: (g, 0, i)),
        compiler_params=pltpu.CompilerParams(vmem_limit_bytes=48 << 20),
        cost_estimate=pl.CostEstimate(
            flops=2 * tokens * depth * features, bytes_accessed=2 * depth * features, transcendentals=0
        ),
        name="project",
    )(*parts, out_weight)


def body(queries, keys, values, key_blocks, block_counts, out_weight):
    tokens = queries.shape[0]
    seq_index = lax.axis_index("seq")
    groups = lax.axis_size("tensor")
    kv_local = keys.shape[1] // HEAD_DIM
    blocks = tokens // BLOCK
    heads = key_blocks.shape[0]
    ratio = heads // kv_local
    slots = lax.dynamic_slice_in_dim(key_blocks, seq_index * blocks, blocks, 1)
    counts = lax.dynamic_slice_in_dim(block_counts, seq_index * blocks, blocks, 1)
    value_t = values.reshape(blocks, BLOCK, kv_local, HEAD_DIM).transpose(2, 0, 3, 1)
    parts = []
    for kv in range(kv_local):
        key_head = lax.all_gather(keys[:, kv * HEAD_DIM : (kv + 1) * HEAD_DIM], "seq", axis=0, tiled=True)
        value_head = lax.all_gather(value_t[kv], "seq", axis=0, tiled=True)
        mine = slice(kv * ratio, (kv + 1) * ratio)
        parts.append(attend(queries, key_head, value_head, slots[mine], counts[mine], kv))
    term = project(parts, out_weight, groups)
    share = lax.psum_scatter(term, "tensor", scatter_dimension=0, tiled=True)
    return share[0]


def solution(mesh):
    placed = (
        P("seq", "tensor"),
        P("seq", "tensor"),
        P("seq", "tensor"),
        P("tensor", None, None),
        P("tensor", None),
        P("tensor", None),
    )
    return jax.shard_map(
        body, mesh=mesh, in_specs=placed, out_specs=P("seq", "tensor"), check_vma=False
    )
```

```python
import functools

import jax
import jax.numpy as jnp
from jax import lax
from jax.experimental import pallas as pl
from jax.experimental.pallas import tpu as pltpu
from jax.sharding import PartitionSpec as P


HEAD_DIM = 128
BLOCK = 128
LOG2E = 1.4426950408889634
NEG = -1e30
PAIR = 2
DEPTHS = (2, 4, 6, 8, 12)
CHUNKS = 4


def attend_kernel(order_ref, count_ref, slot_ref, q_ref, *refs, units, blocks, kmax):
    shards, (o_ref, kv_ref, sems) = refs[:-3], refs[-3:]
    length = shards[0].shape[0]
    v_rows = length // 2
    copies = [
        pltpu.make_async_copy(ref, kv_ref.at[pl.ds(i * length, length), :], sems.at[i])
        for i, ref in enumerate(shards)
    ]
    for copy in copies:
        copy.start()
    for copy in copies:
        copy.wait()
    coef = HEAD_DIM ** (-0.5) * LOG2E
    key_pos = lax.broadcasted_iota(jnp.int32, (BLOCK, BLOCK), 0)
    query_pos = lax.broadcasted_iota(jnp.int32, (BLOCK, BLOCK), 1)
    causal = key_pos <= query_pos

    def run(first, depth):
        sets = []
        for side in range(PAIR):
            unit = order_ref[first + side]
            count = count_ref[unit]
            head = unit // blocks
            block = unit % blocks
            rows = pl.ds(pl.multiple_of(block * BLOCK, BLOCK), BLOCK)
            cols = pl.ds(pl.multiple_of(head * HEAD_DIM, HEAD_DIM), HEAD_DIM)
            own = slot_ref[unit * kmax]
            chosen = [own]
            for slot in range(1, depth):
                chosen.append(jnp.where(slot < count, slot_ref[unit * kmax + slot], own))
            sets.append((count, rows, cols, chosen))
        scored = []
        for count, rows, cols, chosen in sets:
            q = q_ref[rows, cols]
            scores = []
            top = None
            for slot in range(depth):
                start = pl.multiple_of(chosen[slot], BLOCK)
                s = lax.dot_general(
                    kv_ref[pl.ds(start, BLOCK), :], q, (((1,), (1,)), ((), ())),
                    preferred_element_type=jnp.float32,
                )
                if slot == 0:
                    s = jnp.where(causal, s, NEG)
                else:
                    s = jnp.where(slot < count, s, NEG)
                scores.append(s)
                part = jnp.max(s.reshape(BLOCK // 8, 8, BLOCK), axis=0)
                top = part if top is None else jnp.maximum(top, part)
            scored.append((scores, jnp.max(top, axis=0, keepdims=True) * coef))
        for (count, rows, cols, chosen), (scores, top) in zip(sets, scored):
            acc = None
            total = None
            for slot in range(0, depth, 2):
                n = min(2, depth - slot)
                probs = [jnp.exp2(scores[slot + i] * coef - top) for i in range(n)]
                for p in probs:
                    part = jnp.sum(p.reshape(BLOCK // 8, 8, BLOCK), axis=0)
                    total = part if total is None else total + part
                vals = [
                    kv_ref[pl.ds(pl.multiple_of(chosen[slot + i] + v_rows, BLOCK), BLOCK), :]
                    for i in range(n)
                ]
                if n == 2:
                    lhs = jnp.concatenate(vals, axis=1)
                    rhs = jnp.concatenate([p.astype(jnp.bfloat16) for p in probs], axis=0)
                else:
                    lhs, rhs = vals[0], probs[0].astype(jnp.bfloat16)
                term = jnp.dot(lhs, rhs, preferred_element_type=jnp.float32)
                acc = term if acc is None else acc + term
            out = acc / jnp.sum(total, axis=0, keepdims=True)
            o_ref[rows, cols] = out.T.astype(jnp.bfloat16)

    def loop(index, carry):
        first = index * PAIR
        most = count_ref[order_ref[first + PAIR - 1]]
        below = 0
        for depth in [d for d in DEPTHS if d < kmax] + [kmax]:

            @pl.when((most > below) & (most <= depth))
            def _(depth=depth):
                run(first, depth)

            below = depth
        return carry

    lax.fori_loop(0, units // PAIR, loop, 0)


def attend(queries, shards, order, counts, starts, column, chunk, chunks, kmax):
    tokens = queries.shape[0] // chunks
    units = order.shape[0]
    blocks = tokens // BLOCK
    width = units // blocks * HEAD_DIM
    rows = len(shards) * shards[0].shape[0]
    smem = pl.BlockSpec(memory_space=pltpu.SMEM)
    return pl.pallas_call(
        functools.partial(attend_kernel, units=units, blocks=blocks, kmax=kmax),
        out_shape=jax.ShapeDtypeStruct((tokens, width), jnp.bfloat16),
        grid=(1,),
        in_specs=[smem, smem, smem, pl.BlockSpec((tokens, width), lambda i: (chunk, column))]
        + [pl.BlockSpec(memory_space=pl.ANY)] * len(shards),
        out_specs=pl.BlockSpec((tokens, width), lambda i: (0, 0)),
        scratch_shapes=[
            pltpu.VMEM((rows, HEAD_DIM), jnp.bfloat16),
            pltpu.SemaphoreType.DMA((len(shards),)),
        ],
        compiler_params=pltpu.CompilerParams(vmem_limit_bytes=40 << 20),
        cost_estimate=pl.CostEstimate(
            flops=units * kmax * 24 * BLOCK**3, bytes_accessed=rows * 2 * HEAD_DIM, transcendentals=0
        ),
        name="attend",
    )(order, counts, starts, queries, *shards)


def after(value, dep):
    return lax.optimization_barrier((value, dep))[0]


def project_own_kernel(feat_ref, *refs, chunks):
    lhs, (w_ref, o_ref) = refs[:-2], refs[-2:]
    heads = len(lhs) // chunks
    for chunk in range(chunks):
        acc = None
        at = 0
        for ref in lhs[chunk * heads : (chunk + 1) * heads]:
            depth = ref.shape[1]
            term = jnp.dot(ref[...], w_ref[at : at + depth, :], preferred_element_type=jnp.float32)
            acc = term if acc is None else acc + term
            at += depth
        o_ref[chunk] = acc.astype(jnp.bfloat16)


def project_own(parts, out_weight, feats, width):
    flat = [p for chunk in parts for p in chunk]
    tokens = flat[0].shape[0]
    depth = out_weight.shape[0]
    tile = min(512, width)
    per = width // tile
    chunks = len(parts)
    return pl.pallas_call(
        functools.partial(project_own_kernel, chunks=chunks),
        out_shape=jax.ShapeDtypeStruct((chunks, tokens, width), jnp.bfloat16),
        grid_spec=pltpu.PrefetchScalarGridSpec(
            num_scalar_prefetch=1,
            grid=(per,),
            in_specs=[pl.BlockSpec(p.shape, lambda i, f: (0, 0)) for p in flat]
            + [pl.BlockSpec((depth, tile), lambda i, f: (0, f[0] * per + i))],
            out_specs=pl.BlockSpec((chunks, tokens, tile), lambda i, f: (0, 0, i)),
        ),
        compiler_params=pltpu.CompilerParams(vmem_limit_bytes=40 << 20),
        cost_estimate=pl.CostEstimate(
            flops=2 * tokens * chunks * depth * width, bytes_accessed=2 * depth * width, transcendentals=0
        ),
        name="project_own",
    )(feats, *flat, out_weight)


def project_kernel(feat_ref, *refs, lhs_n):
    lhs, w_ref, extra, o_ref = refs[:lhs_n], refs[lhs_n], refs[lhs_n + 1 : -1], refs[-1]
    acc = None
    at = 0
    for ref in lhs:
        depth = ref.shape[1]
        term = jnp.dot(ref[...], w_ref[at : at + depth, :], preferred_element_type=jnp.float32)
        acc = term if acc is None else acc + term
        at += depth
    if extra:
        acc = acc.astype(jnp.bfloat16).astype(jnp.float32)
        for ref in extra:
            acc = acc + ref[0].astype(jnp.float32)
    o_ref[0] = acc.astype(jnp.bfloat16)


def project(parts, out_weight, feats, width, extra=()):
    tokens = parts[0].shape[0]
    depth = out_weight.shape[0]
    n = feats.shape[0]
    tile = min(1024, width)
    per = width // tile
    in_specs = [pl.BlockSpec(p.shape, lambda g, i, f: (0, 0)) for p in parts]
    in_specs.append(pl.BlockSpec((depth, tile), lambda g, i, f: (0, f[g] * per + i)))
    for _, first in extra:
        in_specs.append(pl.BlockSpec((1, tokens, tile), lambda g, i, f, first=first: (g + first, 0, i)))
    return pl.pallas_call(
        functools.partial(project_kernel, lhs_n=len(parts)),
        out_shape=jax.ShapeDtypeStruct((n, tokens, width), jnp.bfloat16),
        grid_spec=pltpu.PrefetchScalarGridSpec(
            num_scalar_prefetch=1,
            grid=(n, per),
            in_specs=in_specs,
            out_specs=pl.BlockSpec((1, tokens, tile), lambda g, i, f: (g, 0, i)),
        ),
        compiler_params=pltpu.CompilerParams(vmem_limit_bytes=40 << 20),
        cost_estimate=pl.CostEstimate(
            flops=2 * tokens * depth * n * width, bytes_accessed=2 * depth * n * width, transcendentals=0
        ),
        name="project",
    )(feats, *parts, out_weight, *[a for a, _ in extra])


def inner(queries, keys, values, key_blocks, block_counts, out_weight):
    tokens = queries.shape[0]
    n_seq = lax.axis_size("seq")
    n_tensor = lax.axis_size("tensor")
    seq_index = lax.axis_index("seq")
    tensor_index = lax.axis_index("tensor")
    kv_local = keys.shape[1] // HEAD_DIM
    blocks = tokens // BLOCK
    heads, _, kmax = key_blocks.shape
    ratio = heads // kv_local
    chunks = CHUNKS
    per = blocks // chunks
    units = ratio * per
    across = 1
    while across * across * 4 <= n_seq:
        across *= 2
    along = n_seq // across

    slots = lax.dynamic_slice_in_dim(key_blocks, seq_index * blocks, blocks, 1)
    counts = lax.dynamic_slice_in_dim(block_counts, seq_index * blocks, blocks, 1)
    shard = slots // blocks
    back_z = (seq_index // across - shard // across + along) % along
    back_x = (seq_index % across - shard % across + across) % across
    starts = ((back_z * across + back_x) * 2 * blocks + slots % blocks) * BLOCK

    def by_chunk(a):
        rest = a.shape[2:]
        a = a.reshape((kv_local, ratio, chunks, per) + rest)
        return jnp.moveaxis(a, 2, 1).reshape((kv_local, chunks, units) + rest)

    counts = by_chunk(counts)
    starts = by_chunk(starts).reshape(kv_local, chunks, units * kmax)
    order = jnp.argsort(counts, axis=2).astype(jnp.int32)

    ring = [
        (z * across + x, (z + 1) % along * across + x) for z in range(along) for x in range(across)
    ]
    value_t = values.reshape(blocks, BLOCK, kv_local, HEAD_DIM).transpose(2, 0, 3, 1)
    swaps = [
        [(z * across + x, z * across + (x + shift) % across) for z in range(along) for x in range(across)]
        for shift in range(1, across)
    ]
    gathered = []
    columns = []
    for kv in range(kv_local):
        own = jnp.concatenate(
            [keys[:, kv * HEAD_DIM : (kv + 1) * HEAD_DIM], value_t[kv].reshape(tokens, HEAD_DIM)], 0
        )
        if kv:
            held = after(own, columns[-1][-1])
            aside = after(own, gathered[-1][-1])
        else:
            held = aside = own
        column = []
        shards = []
        for step in range(along):
            column.append(held)
            shards.append(held)
            for swap in swaps:
                shards.append(lax.ppermute(aside if step == 0 else held, "seq", swap))
            if step < along - 1:
                held = lax.ppermute(held, "seq", ring)
        columns.append(column)
        gathered.append(shards)

    def attended(kv, chunk, dep):
        first = order[kv, chunk] if dep is None else after(order[kv, chunk], dep)
        return attend(
            queries, gathered[kv], first, counts[kv, chunk], starts[kv, chunk], kv, chunk, chunks, kmax
        )

    parts = [[] for _ in range(chunks)]
    for kv in range(kv_local - 1):
        for chunk in range(chunks):
            dep = columns[kv + 1][min(chunk + 1, along - 1)]
            parts[chunk].append(attended(kv, chunk, dep))

    width = out_weight.shape[1] // n_tensor
    rows_y = n_tensor // 2
    core = tensor_index % 2
    pairs = (tensor_index // 2 + jnp.arange(rows_y, dtype=jnp.int32)) % rows_y * 2
    other = pairs + (1 - core)
    mine = pairs + core
    partner = [(t, t ^ 1) for t in range(n_tensor)]
    last = kv_local - 1
    near = [None] * chunks
    terms = [[] for _ in range(chunks)]
    dep = [p for chunk in parts for p in chunk] or None

    def to_rows(chunk, dep):
        terms[chunk].append(near[chunk][0])
        if rows_y == 1:
            return dep
        sums = project(parts[chunk], out_weight, after(mine[1:], dep), width, ((near[chunk], 1),))
        for k in range(1, rows_y):
            there = [(t, (t + 2 * k) % n_tensor) for t in range(n_tensor)]
            terms[chunk].append(lax.ppermute(sums[k - 1], "tensor", there))
        return sums

    for chunk in range(chunks):
        part = attended(last, chunk, dep)
        parts[chunk].append(part)
        dep = part
        if chunk:
            dep = to_rows(chunk - 1, dep)
        half = project(parts[chunk], out_weight, after(other, dep), width)
        near[chunk] = lax.ppermute(half, "tensor", partner)
        dep = half
    dep = to_rows(chunks - 1, dep)
    kept = project_own(parts, out_weight, after(mine[:1], dep), width)
    results = []
    for chunk in range(chunks):
        total = kept[chunk].astype(jnp.float32)
        for term in terms[chunk]:
            total = total + term.astype(jnp.float32)
        results.append(total.astype(jnp.bfloat16))
    return jnp.concatenate(results, 0)


def solution(mesh):
    placed = (
        P("seq", "tensor"),
        P("seq", "tensor"),
        P("seq", "tensor"),
        P("tensor", None, None),
        P("tensor", None),
        P("tensor", None),
    )
    return jax.shard_map(
        inner, mesh=mesh, in_specs=placed, out_specs=P("seq", "tensor"), check_vma=False
    )
```
